32 devices in a mesh: depth: 8 (over z, x), gx: 4 (over y, core).
Axes of the slice: x: 2, y: 2, z: 4, core: 2. Of those that a mesh axis runs over, the one named last changes fastest.
Arguments:
- volume: bfloat16 [64, 192, 2, 512], P(None, 'depth', None, 'gx'), may hold values from -6 to 6
- conv_first: bfloat16 [3, 3, 3, 64, 64], replicated, may hold values from -0.15625 to 0.15625
- conv_second: bfloat16 [3, 3, 3, 64, 64], replicated, may hold values from -0.15625 to 0.15625
- mode_weights: bfloat16 [64, 64, 64], P('depth'), may hold values from -0.75 to 0.75
Outputs:
- next_volume: bfloat16 [64, 192, 2, 512], P(None, 'depth', None, 'gx')
The draws below stay inside these ranges and needn't reach their ends.
All inputs are finite; a program needn't handle non-finite values.
Results may differ from the reference program's by a relative error of at most 0.01.
Values may be sent and summed in bfloat16 or wider, within the bound.
No kernel may reach another device: no remote copies, remote signals or barrier semaphores. Data moves between devices by JAX's collectives and lax.ppermute only.
A program may use at most 64 MiB of HBM per device.

```python
import math
import jax
import jax.numpy as jnp
from jax import lax

C = 64
MODES = 32
CD = 24
NY = 2
NZ = 192
NX = 512
N_DEPTH = 8


def levels(key, dims, split, low, high):
    def one(position, parts):
        steps = jax.random.uniform(jax.random.fold_in(jax.random.fold_in(key, 6), position), (parts,), jnp.float32, low / len(split), high / len(split))
        return jnp.repeat(jnp.exp(steps), dims[position] // parts).reshape((-1,) + (1,) * (len(dims) - position - 1))

    factor_of = one(*split[0])
    for cut in split[1:]:
        factor_of = factor_of * one(*cut)
    return factor_of


def scatter_about(own_key, extent, scale, limit, pieces=(), kind=jnp.bfloat16):
    gain = levels(own_key, extent, pieces, -0.22, 0.18) if pieces else 1.0
    array = jax.random.normal(own_key, extent, jnp.float32) * scale * gain
    return jnp.minimum(jnp.maximum(array, -limit), limit).astype(kind)


def setup_inputs(seed: int = 0) -> dict:
    seeds = jax.random.split(jax.random.key(seed), 5)
    return {
        "volume": scatter_about(seeds[0], (C, NZ, NY, NX), 1.0, 6.0, ((1, 8), (3, 4))),
        "conv_first": scatter_about(seeds[1], (3, 3, 3, C, C), (27 * C) ** -0.5, 0.15625),
        "conv_second": scatter_about(seeds[2], (3, 3, 3, C, C), (27 * C) ** -0.5, 0.15625),
        "mode_weights": scatter_about(seeds[3], (2 * MODES, C, C), C ** -0.5, 0.75, ((0, 8),)),
    }


def mode_basis(mode_index, depth_pos, total_z):
    frequency = jnp.where(mode_index < MODES, mode_index, mode_index - MODES + 1).astype(jnp.float32)
    odd_steps = (2 * depth_pos + 1).astype(jnp.float32)
    angles = frequency[:, None] * odd_steps[None, :] * (math.pi / (2.0 * total_z))
    values = jnp.where((mode_index < MODES)[:, None], jnp.cos(angles), jnp.sin(angles))
    return (values * math.sqrt(2.0 / total_z)).astype(jnp.bfloat16)

def convolve(source, weights):
    kernel = jnp.transpose(weights.astype(jnp.float32), (3, 4, 0, 1, 2))
    result = lax.conv_general_dilated(source[None].astype(jnp.float32), kernel, (1, 1, 1), 'SAME', dimension_numbers=('NCDHW', 'OIDHW', 'NCDHW'), precision=lax.Precision.HIGHEST)
    return result[0]

def reference(volume, conv_first, conv_second, mode_weights):
    hidden = jax.nn.gelu(convolve(volume, conv_first)).astype(jnp.bfloat16)
    local_part = convolve(hidden, conv_second)
    mode_index = jnp.arange(2 * MODES, dtype=jnp.int32)

    def shard_term(running, shard_index):
        depth_pos = shard_index * CD + jnp.arange(CD, dtype=jnp.int32)
        slab = lax.dynamic_slice_in_dim(volume, (shard_index * CD).astype(jnp.int32), CD, 1)
        partial_term = jnp.einsum('mz,czyx->mcyx', mode_basis(mode_index, depth_pos, NZ).astype(jnp.float32), slab.astype(jnp.float32), precision=lax.Precision.HIGHEST)
        rounded = lax.optimization_barrier(partial_term.astype(jnp.bfloat16))
        return (running + rounded.astype(jnp.float32), None)
    start_sum = jnp.zeros((2 * MODES, C, NY, volume.shape[3]), jnp.float32)
    summed, _ = lax.scan(shard_term, start_sum, jnp.arange(N_DEPTH, dtype=jnp.int32))
    coefficients = summed.astype(jnp.bfloat16)
    mixed = jnp.einsum('moc,mcyx->moyx', mode_weights.astype(jnp.float32), coefficients.astype(jnp.float32), precision=lax.Precision.HIGHEST).astype(jnp.bfloat16)
    full_basis = mode_basis(mode_index, jnp.arange(NZ, dtype=jnp.int32), NZ).astype(jnp.float32)
    spectral = jnp.einsum('mz,mcyx->czyx', full_basis, mixed.astype(jnp.float32), precision=lax.Precision.HIGHEST)
    return (volume.astype(jnp.float32) + local_part + spectral).astype(jnp.bfloat16)
```

```python
import math

import jax
import jax.numpy as jnp
from jax import lax
from jax.experimental import pallas as pl
from jax.experimental.pallas import tpu as pltpu
from jax.sharding import PartitionSpec as P

MODES = 32
BF = jnp.bfloat16
F32 = jnp.float32
VMEM = pl.BlockSpec(memory_space=pltpu.VMEM)
SMEM = pl.BlockSpec(memory_space=pltpu.SMEM)


def mode_basis(mode_index, depth_pos, total_z):
    frequency = jnp.where(mode_index < MODES, mode_index, mode_index - MODES + 1).astype(F32)
    odd_steps = (2 * depth_pos + 1).astype(F32)
    angles = frequency[:, None] * odd_steps[None, :] * (math.pi / (2.0 * total_z))
    values = jnp.where((mode_index < MODES)[:, None], jnp.cos(angles), jnp.sin(angles))
    return (values * math.sqrt(2.0 / total_z)).astype(BF)


def cost(flops, nbytes, trans=0):
    return pl.CostEstimate(flops=flops, bytes_accessed=nbytes, transcendentals=trans)


def params():
    return pltpu.CompilerParams(vmem_limit_bytes=60 * 1024 * 1024)


def split_kernel(place, field, weights, vt, *chunks):
    pairs, lanes, cols = field.shape
    n = len(chunks)
    part = cols // n
    half = lanes // 2
    own = weights.shape[0] // 2
    wide = weights.shape[2] * 2
    core = place[n]
    for q in range(pairs):
        vt[q] = field[q].T
    body = 2 * pairs * part
    for k in range(n):
        start = pl.multiple_of(place[k] * part, part)
        for q in range(pairs):
            for par in range(2):
                chunks[k][pl.ds((par * pairs + q) * part, part), :] = vt[
                    q, pl.ds(start, part), pl.ds(par * half, half)
                ]
        for j in range(own // 2):
            first = weights[core * own + 2 * j]
            second = weights[core * own + 2 * j + 1]
            rows = weights.shape[1]
            chunks[k][pl.ds(body + j * rows, rows), :] = jnp.concatenate([first, second], axis=1)


def taps_kernel(first, second, out_first, out_second):
    ch = first.shape[3]
    for src, dst in ((first, out_first), (second, out_second)):
        for e in range(3):
            block = {}
            for a in range(3):
                for yi in range(2):
                    both = jnp.concatenate([src[a, yi + 1, e], src[a, yi, e]], axis=0)
                    block[a, yi] = both.astype(F32).T.astype(BF)
            for h in range(2):
                for pi in range(2):
                    for po in range(2):
                        a = 2 * h + pi - po
                        for yi in range(2):
                            value = block[a, yi] if 0 <= a <= 2 else jnp.zeros((ch, 2 * ch), BF)
                            dst[
                                e * 2 + h,
                                pl.ds((pi * 2 + yi) * ch, ch),
                                pl.ds(po * 2 * ch, 2 * ch),
                            ] = value


def shifted(dst, index, rows, value):
    n = value.shape[0]
    wide = value.astype(F32)
    dst[1, pl.ds(index * rows, rows), :] = value
    dst[0, pl.ds(index * rows, rows), :] = pltpu.roll(wide, 1, 0).astype(BF)
    dst[2, pl.ds(index * rows, rows), :] = pltpu.roll(wide, n - 1, 0).astype(BF)


def conv_kernel(edge, vt, before, after, left, right, w1, w2, out, ext, hid):
    pairs, cols, lanes = vt.shape
    rows = cols + 16
    fill = jnp.zeros((rows - cols - 4, lanes), F32)
    for q in range(pairs + 2):
        mid = before[...] if q == 0 else after[...] if q == pairs + 1 else vt[q - 1]
        ring = jnp.concatenate(
            [mid.astype(F32), right[q].astype(F32), fill, left[q].astype(F32)], axis=0
        ).astype(BF)
        shifted(ext, q, rows, ring)
    at = lax.broadcasted_iota(jnp.int32, (rows, lanes), 0)
    lane = lax.broadcasted_iota(jnp.int32, (rows, lanes), 1)
    inside = jnp.logical_and(
        jnp.logical_or(at != rows - 1, edge[2] != 0), jnp.logical_or(at != cols, edge[3] != 0)
    )
    for p in range(pairs + 1):
        acc = jnp.zeros((rows, lanes), F32)
        for e in range(3):
            for h in range(2):
                acc += jnp.dot(
                    ext[e, pl.ds((p + h) * rows, rows), :],
                    w1[e * 2 + h],
                    preferred_element_type=F32,
                )
        keep = inside
        if p == 0:
            keep = jnp.logical_and(keep, jnp.logical_or(lane >= lanes // 2, edge[0] != 0))
        if p == pairs:
            keep = jnp.logical_and(keep, jnp.logical_or(lane < lanes // 2, edge[1] != 0))
        value = jnp.where(keep, jax.nn.gelu(acc), 0.0).astype(BF)
        shifted(hid, p, rows, value)
    for p in range(pairs):
        acc = jnp.zeros((cols, lanes), F32)
        for e in range(3):
            for h in range(2):
                acc += jnp.dot(
                    hid[e, pl.ds((p + h) * rows, cols), :],
                    w2[e * 2 + h],
                    preferred_element_type=F32,
                )
        out[p] = acc


def spectral_kernel(basis, basis_t, other, *refs):
    n = other.shape[0]
    chunks, outs = refs[:n], refs[n : 2 * n]
    field, coef, mix = refs[2 * n :]
    modes = basis.shape[0]
    wide = other.shape[2]
    ch = wide // 2
    per = field.shape[1] // n
    body = 2 * per
    steps = basis.shape[1] // 2
    part = field.shape[1] // steps
    for k in range(n):
        for par in range(2):
            field[par, pl.ds(k * per, per), :] = chunks[k][pl.ds(par * per, per), :].astype(F32)
    for x in range(part):
        piece = jnp.concatenate(
            [field[par, pl.ds(x, steps, stride=part), :].astype(BF) for par in range(2)], axis=0
        )
        coef[pl.ds(x, modes, stride=part), :] = jnp.dot(
            basis[...], piece, preferred_element_type=F32
        )
    low = lax.broadcasted_iota(jnp.int32, (part, wide), 1) < ch
    duo = modes // 2 // (2 * n)
    at = 0
    for side in range(2):
        for k in range(n):
            for j in range(duo):
                if side == 0:
                    w = chunks[k][pl.ds(body + j * ch, ch), :]
                else:
                    w = other[k, pl.ds(j * ch, ch), :]
                c0 = coef[pl.ds(at * part, part), :]
                c1 = coef[pl.ds((at + 1) * part, part), :]
                lhs = jnp.concatenate(
                    [
                        jnp.where(low, c0, 0.0),
                        jnp.where(low, pltpu.roll(c0, ch, 1), 0.0),
                        jnp.where(low, 0.0, pltpu.roll(c1, ch, 1)),
                        jnp.where(low, 0.0, c1),
                    ],
                    axis=0,
                ).astype(BF)
                r = lax.dot_general(
                    lhs, w, (((1,), (1,)), ((), ())), preferred_element_type=F32
                )
                for t in range(2):
                    mix[pl.ds((at + t) * part, part), :] = jnp.concatenate(
                        [
                            r[2 * t * part : (2 * t + 1) * part],
                            r[(2 * t + 1) * part : (2 * t + 2) * part],
                        ],
                        axis=1,
                    )
                at += 2
    for x in range(part):
        value = jnp.dot(
            basis_t[...],
            mix[pl.ds(x, modes, stride=part), :].astype(BF),
            preferred_element_type=F32,
        )
        for par in range(2):
            field[par, pl.ds(x, steps, stride=part), :] = value[par * steps : (par + 1) * steps]
    for k in range(n):
        for par in range(2):
            outs[k][pl.ds(par * per, per), :] = field[par, pl.ds(k * per, per), :].astype(BF)


def join_kernel(place, field, local_part, *refs):
    pairs, lanes, cols = field.shape
    n = len(refs) - 2
    chunks, out, total = refs[:n], refs[n], refs[n + 1]
    part = cols // n
    half = lanes // 2
    for k in range(n):
        start = pl.multiple_of(place[k] * part, part)
        for q in range(pairs):
            for par in range(2):
                total[q, pl.ds(start, part), pl.ds(par * half, half)] = chunks[k][
                    pl.ds((par * pairs + q) * part, part), :
                ].astype(F32)
    for q in range(pairs):
        value = (total[q] + local_part[q]).T
        out[q] = (field[q].astype(F32) + value).astype(BF)


def shift_line(value, axis, step):
    count = lax.axis_size(axis)
    pairs = [(i, i + step) for i in range(count) if 0 <= i + step < count]
    return lax.ppermute(value, axis, pairs)


def local(volume, conv_first, conv_second, mode_weights):
    ch, slab, ny, cols = volume.shape
    n = lax.axis_size("depth")
    ngx = lax.axis_size("gx")
    total_z = slab * n
    pairs = slab // 2
    lanes = 2 * ny * ch
    part = cols // n
    per = pairs * part
    modes = mode_weights.shape[0] * n
    me = lax.axis_index("depth")
    gx = lax.axis_index("gx")
    core = gx % 2
    own = mode_weights.shape[0] // 2
    twofold = n & (n - 1) == 0
    ks = jnp.arange(n, dtype=jnp.int32)
    to = (me ^ ks) if twofold else (me + ks) % n
    source = to if twofold else (me - ks) % n

    def send(value, k, back=False):
        if k == 0:
            return value
        if twofold:
            table = [(i, i ^ k) for i in range(n)]
        else:
            table = [(i, (i - k if back else i + k) % n) for i in range(n)]
        return lax.ppermute(value, "depth", table)

    field = jnp.transpose(volume, (1, 2, 0, 3)).reshape(pairs, lanes, cols)
    place = jnp.concatenate([to, core[None]]).astype(jnp.int32)
    wrows = own // 2 * ch
    vt, *chunks = pl.pallas_call(
        split_kernel,
        out_shape=[jax.ShapeDtypeStruct((pairs, cols, lanes), BF)]
        + [jax.ShapeDtypeStruct((2 * per + wrows, lanes // 2), BF)] * n,
        in_specs=[SMEM, VMEM, VMEM],
        out_specs=[VMEM] * (n + 1),
        compiler_params=params(),
        cost_estimate=cost(0, 3 * volume.size * 2),
    )(place, field, mode_weights)
    got = [send(chunks[k], k) for k in range(n)]

    w1, w2 = pl.pallas_call(
        taps_kernel,
        out_shape=[jax.ShapeDtypeStruct((6, lanes, lanes), BF)] * 2,
        in_specs=[VMEM, VMEM],
        out_specs=[VMEM, VMEM],
        compiler_params=params(),
        cost_estimate=cost(0, 4 * conv_first.size * 2 * 4),
    )(conv_first, conv_second)

    before = shift_line(vt[pairs - 1], "depth", 1)
    after = shift_line(vt[0], "depth", -1)

    def strip(at):
        return jnp.concatenate(
            [before[None, at : at + 2], vt[:, at : at + 2], after[None, at : at + 2]], axis=0
        )

    left = shift_line(strip(cols - 2), "gx", 1)
    right = shift_line(strip(0), "gx", -1)

    mine = jnp.stack([g[2 * per :] for g in got])
    other = lax.ppermute(mine, "gx", [(i, i ^ 1) for i in range(ngx)])
    inner = jnp.arange(own, dtype=jnp.int32)[None, :] + source[:, None] * (2 * own)
    ids = jnp.concatenate(
        [(inner + core * own).reshape(-1), (inner + (1 - core) * own).reshape(-1)]
    )
    depth_pos = (
        jnp.arange(2, dtype=jnp.int32)[:, None, None]
        + source[None, :, None] * slab
        + 2 * jnp.arange(pairs, dtype=jnp.int32)[None, None, :]
    ).reshape(-1)
    basis = mode_basis(ids, depth_pos, total_z)
    outs = pl.pallas_call(
        spectral_kernel,
        out_shape=[jax.ShapeDtypeStruct((2 * per, lanes // 2), BF)] * n,
        in_specs=[VMEM] * (3 + n),
        out_specs=[VMEM] * n,
        scratch_shapes=[
            pltpu.VMEM((2, n * per, lanes // 2), F32),
            pltpu.VMEM((modes * part, lanes // 2), F32),
            pltpu.VMEM((modes * part, lanes // 2), F32),
        ],
        compiler_params=params(),
        cost_estimate=cost(4 * modes * total_z * part * lanes // 2, 3 * volume.size * 2),
    )(basis, basis.T, other, *got)
    spec = [send(outs[k], k, True) for k in range(n)]

    edge = jnp.stack([me > 0, me < n - 1, gx > 0, gx < ngx - 1]).astype(jnp.int32)
    local_part = pl.pallas_call(
        conv_kernel,
        out_shape=jax.ShapeDtypeStruct((pairs, cols, lanes), F32),
        in_specs=[SMEM] + [VMEM] * 7,
        out_specs=VMEM,
        scratch_shapes=[
            pltpu.VMEM((3, (pairs + 2) * (cols + 16), lanes), BF),
            pltpu.VMEM((3, (pairs + 1) * (cols + 16), lanes), BF),
        ],
        compiler_params=params(),
        cost_estimate=cost(4 * 6 * pairs * cols * lanes * lanes, volume.size * 8),
    )(edge, vt, before, after, left, right, w1, w2)

    out = pl.pallas_call(
        join_kernel,
        out_shape=jax.ShapeDtypeStruct((pairs, lanes, cols), BF),
        in_specs=[SMEM] + [VMEM] * (2 + n),
        out_specs=VMEM,
        scratch_shapes=[pltpu.VMEM((pairs, cols, lanes), F32)],
        compiler_params=params(),
        cost_estimate=cost(0, volume.size * 10),
    )(to.astype(jnp.int32), field, local_part, *spec)
    return jnp.transpose(out.reshape(slab, ny, ch, cols), (2, 0, 1, 3))


def solution(mesh):
    placed = (P(None, "depth", None, "gx"), P(), P(), P("depth", None, None))
    return jax.shard_map(
        local, mesh=mesh, in_specs=placed, out_specs=P(None, "depth", None, "gx"), check_vma=False
    )
```

```python
import functools
import math

import jax
import jax.numpy as jnp
from jax import lax
from jax.experimental import pallas as pl
from jax.experimental.pallas import tpu as pltpu
from jax.sharding import PartitionSpec as P


MODES = 32
BF = jnp.bfloat16
F32 = jnp.float32
VMEM = pl.BlockSpec(memory_space=pltpu.VMEM)


def mode_basis(mode_index, depth_pos, total_z):
    frequency = jnp.where(mode_index < MODES, mode_index, mode_index - MODES + 1).astype(F32)
    odd_steps = (2 * depth_pos + 1).astype(F32)
    angles = frequency[:, None] * odd_steps[None, :] * (math.pi / (2.0 * total_z))
    values = jnp.where((mode_index < MODES)[:, None], jnp.cos(angles), jnp.sin(angles))
    return (values * math.sqrt(2.0 / total_z)).astype(BF)


def cost(flops, nbytes, trans=0):
    return pl.CostEstimate(flops=flops, bytes_accessed=nbytes, transcendentals=trans)


def params():
    return pltpu.CompilerParams(vmem_limit_bytes=20 * 1024 * 1024)


def target(n, k):
    me = lax.axis_index("depth")
    return me ^ k if n & (n - 1) == 0 else (me + k) % n


def split_kernel(slab, flat, weights, vt, *refs):
    *chunks, wide = refs
    pairs, cols, lanes = vt.shape
    n = len(chunks)
    part = cols // n
    half = lanes // 2
    own = weights.shape[0] // 2
    ch = weights.shape[2]
    stride = flat.shape[0] // ch
    ny = stride // slab
    core = lax.axis_index("gx") % 2
    wide[...] = flat[...].astype(F32)
    for q in range(pairs):
        rows = [wide[pl.ds(2 * q * ny + j, ch, stride=stride), :] for j in range(2 * ny)]
        vt[q] = jnp.concatenate(rows, axis=0).astype(BF).T
    body = 2 * pairs * part
    for k in range(n):
        start = pl.multiple_of(target(n, k) * part, part)
        for q in range(pairs):
            for par in range(2):
                chunks[k][pl.ds((par * pairs + q) * part, part), :] = vt[
                    q, pl.ds(start, part), pl.ds(par * half, half)
                ]
        for j in range(own // 2):
            first = weights[core * own + 2 * j]
            second = weights[core * own + 2 * j + 1]
            chunks[k][pl.ds(body + j * ch, ch), :] = jnp.concatenate([first, second], axis=1)


def taps_kernel(first, second, out_first, out_second):
    ch = first.shape[3]
    for src, dst in ((first, out_first), (second, out_second)):
        for e in range(3):
            block = {}
            for a in range(3):
                for yi in range(2):
                    both = jnp.concatenate([src[a, yi + 1, e], src[a, yi, e]], axis=0)
                    block[a, yi] = both.astype(F32).T.astype(BF)
            for h in range(2):
                for pi in range(2):
                    for po in range(2):
                        a = 2 * h + pi - po
                        for yi in range(2):
                            value = block[a, yi] if 0 <= a <= 2 else jnp.zeros((ch, 2 * ch), BF)
                            dst[
                                e * 2 + h,
                                pl.ds((pi * 2 + yi) * ch, ch),
                                pl.ds(po * 2 * ch, 2 * ch),
                            ] = value


def shifted(dst, index, rows, value):
    n = value.shape[0]
    wide = value.astype(F32)
    dst[1, pl.ds(index * rows, rows), :] = value
    dst[0, pl.ds(index * rows, rows), :] = pltpu.roll(wide, 1, 0).astype(BF)
    dst[2, pl.ds(index * rows, rows), :] = pltpu.roll(wide, n - 1, 0).astype(BF)


def conv_kernel(ngx, n, flat, vt, before, after, left, right, w1, w2, out, ext, hid):
    pairs, cols, lanes = vt.shape
    rows = cols + 16
    stride = 4 * flat.shape[0] // lanes
    ch = lanes // 4
    me = lax.axis_index("depth")
    gx = lax.axis_index("gx")
    fill = jnp.zeros((rows - cols - 4, lanes), F32)
    for q in range(pairs + 2):
        if 0 < q < pairs + 1:
            mid, lo, hi = vt[q - 1], left[q - 1], right[q - 1]
        else:
            end = before if q == 0 else after
            mid, lo, hi = end[pl.ds(0, cols), :], end[pl.ds(cols + 2, 2), :], end[pl.ds(cols, 2), :]
        ring = jnp.concatenate(
            [mid.astype(F32), hi.astype(F32), fill, lo.astype(F32)], axis=0
        ).astype(BF)
        shifted(ext, q, rows, ring)
    at = lax.broadcasted_iota(jnp.int32, (rows, lanes), 0)
    lane = lax.broadcasted_iota(jnp.int32, (rows, lanes), 1)
    inside = jnp.logical_and(
        jnp.logical_or(at != rows - 1, gx > 0), jnp.logical_or(at != cols, gx < ngx - 1)
    )
    for p in range(pairs + 1):
        acc = jnp.zeros((rows, lanes), F32)
        for e in range(3):
            for h in range(2):
                acc += jnp.dot(
                    ext[e, pl.ds((p + h) * rows, rows), :],
                    w1[e * 2 + h],
                    preferred_element_type=F32,
                )
        keep = inside
        if p == 0:
            keep = jnp.logical_and(keep, jnp.logical_or(lane >= lanes // 2, me > 0))
        if p == pairs:
            keep = jnp.logical_and(keep, jnp.logical_or(lane < lanes // 2, me < n - 1))
        value = jnp.where(keep, jax.nn.gelu(acc), 0.0).astype(BF)
        shifted(hid, p, rows, value)
    for p in range(pairs):
        acc = jnp.zeros((cols, lanes), F32)
        for e in range(3):
            for h in range(2):
                acc += jnp.dot(
                    hid[e, pl.ds((p + h) * rows, cols), :],
                    w2[e * 2 + h],
                    preferred_element_type=F32,
                )
        turned = acc.T
        for j in range(4):
            out[pl.ds(4 * p + j, ch, stride=stride), :] = turned[j * ch : (j + 1) * ch]
    out[...] += flat[...].astype(F32)


def spectral_kernel(basis, basis_t, other, *refs):
    n = other.shape[0]
    chunks, outs = refs[:n], refs[n : 2 * n]
    field, coef, mix = refs[2 * n :]
    modes = basis.shape[0]
    wide = other.shape[2]
    ch = wide // 2
    per = field.shape[1] // n
    body = 2 * per
    steps = basis.shape[1] // 2
    part = field.shape[1] // steps
    for k in range(n):
        for par in range(2):
            field[par, pl.ds(k * per, per), :] = chunks[k][pl.ds(par * per, per), :].astype(F32)
    for x in range(part):
        piece = jnp.concatenate(
            [field[par, pl.ds(x, steps, stride=part), :].astype(BF) for par in range(2)], axis=0
        )
        coef[pl.ds(x, modes, stride=part), :] = jnp.dot(
            basis[...], piece, preferred_element_type=F32
        )
    low = lax.broadcasted_iota(jnp.int32, (part, wide), 1) < ch
    duo = modes // 2 // (2 * n)
    at = 0
    for side in range(2):
        for k in range(n):
            for j in range(duo):
                if side == 0:
                    w = chunks[k][pl.ds(body + j * ch, ch), :]
                else:
                    w = other[k, pl.ds(j * ch, ch), :]
                c0 = coef[pl.ds(at * part, part), :]
                c1 = coef[pl.ds((at + 1) * part, part), :]
                lhs = jnp.concatenate(
                    [
                        jnp.where(low, c0, 0.0),
                        jnp.where(low, pltpu.roll(c0, ch, 1), 0.0),
                        jnp.where(low, 0.0, pltpu.roll(c1, ch, 1)),
                        jnp.where(low, 0.0, c1),
                    ],
                    axis=0,
                ).astype(BF)
                r = lax.dot_general(
                    lhs, w, (((1,), (1,)), ((), ())), preferred_element_type=F32
                )
                for t in range(2):
                    mix[pl.ds((at + t) * part, part), :] = jnp.concatenate(
                        [
                            r[2 * t * part : (2 * t + 1) * part],
                            r[(2 * t + 1) * part : (2 * t + 2) * part],
                        ],
                        axis=1,
                    )
                at += 2
    for x in range(part):
        value = jnp.dot(
            basis_t[...],
            mix[pl.ds(x, modes, stride=part), :].astype(BF),
            preferred_element_type=F32,
        )
        for par in range(2):
            field[par, pl.ds(x, steps, stride=part), :] = value[par * steps : (par + 1) * steps]
    for k in range(n):
        for par in range(2):
            outs[k][pl.ds(par * per, per), :] = field[par, pl.ds(k * per, per), :].astype(BF)


def join_kernel(base, *refs):
    *chunks, out, total, wide = refs
    pairs, cols, lanes = total.shape
    n = len(chunks)
    part = cols // n
    half = lanes // 2
    stride = 4 * base.shape[0] // lanes
    ch = lanes // 4
    for k in range(n):
        start = pl.multiple_of(target(n, k) * part, part)
        for q in range(pairs):
            for par in range(2):
                total[q, pl.ds(start, part), pl.ds(par * half, half)] = chunks[k][
                    pl.ds((par * pairs + q) * part, part), :
                ]
    for q in range(pairs):
        turned = total[q].T.astype(F32)
        for j in range(4):
            wide[pl.ds(4 * q + j, ch, stride=stride), :] = turned[j * ch : (j + 1) * ch]
    out[...] = (base[...] + wide[...]).astype(BF)


def shift_line(value, axis, step):
    count = lax.axis_size(axis)
    pairs = [(i, i + step) for i in range(count) if 0 <= i + step < count]
    return lax.ppermute(value, axis, pairs)


def block(volume, conv_first, conv_second, mode_weights):
    ch, slab, ny, cols = volume.shape
    n = lax.axis_size("depth")
    ngx = lax.axis_size("gx")
    total_z = slab * n
    pairs = slab // 2
    lanes = 2 * ny * ch
    part = cols // n
    per = pairs * part
    modes = mode_weights.shape[0] * n
    me = lax.axis_index("depth")
    core = lax.axis_index("gx") % 2
    own = mode_weights.shape[0] // 2
    twofold = n & (n - 1) == 0
    ks = jnp.arange(n, dtype=jnp.int32)
    source = me ^ ks if twofold else (me - ks) % n

    def send(value, k, back=False):
        if k == 0:
            return value
        if twofold:
            table = [(i, i ^ k) for i in range(n)]
        else:
            table = [(i, (i - k if back else i + k) % n) for i in range(n)]
        return lax.ppermute(value, "depth", table)

    flat = volume.reshape(ch * slab * ny, cols)
    wrows = own // 2 * ch
    vt, *chunks = pl.pallas_call(
        functools.partial(split_kernel, slab),
        out_shape=[jax.ShapeDtypeStruct((pairs, cols, lanes), BF)]
        + [jax.ShapeDtypeStruct((2 * per + wrows, lanes // 2), BF)] * n,
        in_specs=[VMEM, VMEM],
        out_specs=[VMEM] * (n + 1),
        scratch_shapes=[pltpu.VMEM(flat.shape, F32)],
        compiler_params=params(),
        cost_estimate=cost(0, 3 * volume.size * 2),
    )(flat, mode_weights)
    got = [send(chunks[k], k) for k in range(n)]

    left = shift_line(vt[:, cols - 2 :], "gx", 1)
    right = shift_line(vt[:, :2], "gx", -1)
    last = jnp.concatenate([vt[pairs - 1], right[pairs - 1], left[pairs - 1]], axis=0)
    before = shift_line(last, "depth", 1)
    first = jnp.concatenate([vt[0], right[0], left[0]], axis=0)
    after = shift_line(first, "depth", -1)

    w1, w2 = pl.pallas_call(
        taps_kernel,
        out_shape=[jax.ShapeDtypeStruct((6, lanes, lanes), BF)] * 2,
        in_specs=[VMEM, VMEM],
        out_specs=[VMEM, VMEM],
        compiler_params=params(),
        cost_estimate=cost(0, 4 * conv_first.size * 2 * 4),
    )(conv_first, conv_second)

    mine = jnp.stack([g[2 * per :] for g in got])
    other = lax.ppermute(mine, "gx", [(i, i ^ 1) for i in range(ngx)])
    inner = jnp.arange(own, dtype=jnp.int32)[None, :] + source[:, None] * (2 * own)
    ids = jnp.concatenate(
        [(inner + core * own).reshape(-1), (inner + (1 - core) * own).reshape(-1)]
    )
    depth_pos = (
        jnp.arange(2, dtype=jnp.int32)[:, None, None]
        + source[None, :, None] * slab
        + 2 * jnp.arange(pairs, dtype=jnp.int32)[None, None, :]
    ).reshape(-1)
    basis = mode_basis(ids, depth_pos, total_z)
    outs = pl.pallas_call(
        spectral_kernel,
        out_shape=[jax.ShapeDtypeStruct((2 * per, lanes // 2), BF)] * n,
        in_specs=[VMEM] * (3 + n),
        out_specs=[VMEM] * n,
        scratch_shapes=[
            pltpu.VMEM((2, n * per, lanes // 2), F32),
            pltpu.VMEM((modes * part, lanes // 2), F32),
            pltpu.VMEM((modes * part, lanes // 2), F32),
        ],
        compiler_params=params(),
        cost_estimate=cost(4 * modes * total_z * part * lanes // 2, 3 * volume.size * 2),
    )(basis, basis.T, other, *got)
    spec = [send(outs[k], k, True) for k in range(n)]

    base = pl.pallas_call(
        functools.partial(conv_kernel, ngx, n),
        out_shape=jax.ShapeDtypeStruct(flat.shape, F32),
        in_specs=[VMEM] * 8,
        out_specs=VMEM,
        scratch_shapes=[
            pltpu.VMEM((3, (pairs + 2) * (cols + 16), lanes), BF),
            pltpu.VMEM((3, (pairs + 1) * (cols + 16), lanes), BF),
        ],
        compiler_params=params(),
        cost_estimate=cost(4 * 6 * pairs * cols * lanes * lanes, volume.size * 8),
    )(flat, vt, before, after, left, right, w1, w2)

    out = pl.pallas_call(
        join_kernel,
        out_shape=jax.ShapeDtypeStruct(flat.shape, BF),
        in_specs=[VMEM] * (1 + n),
        out_specs=VMEM,
        scratch_shapes=[pltpu.VMEM((pairs, cols, lanes), BF), pltpu.VMEM(flat.shape, F32)],
        compiler_params=params(),
        cost_estimate=cost(0, volume.size * 10),
    )(base, *spec)
    return out.reshape(volume.shape)


def solution(mesh):
    placed = (P(None, "depth", None, "gx"), P(), P(), P("depth", None, None))
    return jax.shard_map(
        block, mesh=mesh, in_specs=placed, out_specs=P(None, "depth", None, "gx"), check_vma=False
    )
```

```python
import functools
import math

import jax
import jax.numpy as jnp
from jax import lax
from jax.experimental import pallas as pl
from jax.experimental.pallas import tpu as pltpu
from jax.sharding import PartitionSpec as P


MODES = 32
BF = jnp.bfloat16
F32 = jnp.float32
VMEM = pl.BlockSpec(memory_space=pltpu.VMEM)
HBM = pl.BlockSpec(memory_space=pltpu.HBM)


def mode_basis(mode_index, depth_pos, total_z):
    frequency = jnp.where(mode_index < MODES, mode_index, mode_index - MODES + 1).astype(F32)
    odd_steps = (2 * depth_pos + 1).astype(F32)
    angles = frequency * odd_steps * (math.pi / (2.0 * total_z))
    values = jnp.where(mode_index < MODES, jnp.cos(angles), jnp.sin(angles))
    return values * math.sqrt(2.0 / total_z)


def cost(flops, nbytes, trans=0):
    return pl.CostEstimate(flops=flops, bytes_accessed=nbytes, transcendentals=trans)


def in_hbm(value):
    return pltpu.with_memory_space_constraint(value, pltpu.HBM)


def params():
    return pltpu.CompilerParams(vmem_limit_bytes=20 * 1024 * 1024)


def target(k):
    me = lax.axis_index("depth")
    return me ^ k


def split_kernel(slab, flat, weights, vt, odd, *refs):
    *chunks, held, modes, wide, sem = refs
    pairs, cols, lanes = vt.shape
    n = len(chunks)
    part = cols // n
    half = lanes // 2
    own = weights.shape[0] // 2
    ch = weights.shape[2]
    stride = flat.shape[0] // ch
    ny = stride // slab
    core = lax.axis_index("gx") % 2
    upper = lax.axis_index("depth") % 2
    block = flat.shape[0] // 4
    loads = [
        pltpu.make_async_copy(
            flat.at[pl.ds(i * block, block), :], held.at[pl.ds(i * block, block), :], sem.at[i]
        )
        for i in range(4)
    ]
    loads.append(pltpu.make_async_copy(weights.at[pl.ds(core * own, own)], modes, sem.at[4]))
    for load in loads:
        load.start()
    for i in range(4):
        loads[i].wait()
        wide[pl.ds(i * block, block), :] = held[pl.ds(i * block, block), :].astype(F32)
    for q in range(pairs):
        rows = [wide[pl.ds(2 * q * ny + j, ch, stride=stride), :] for j in range(2 * ny)]
        vt[q] = jnp.concatenate(rows, axis=0).astype(BF).T
    body = 2 * pairs * part
    loads[4].wait()
    for k in range(n):
        start = pl.multiple_of(target(k) * part, part)
        for q in range(pairs):
            for par in range(2):
                chunks[k][pl.ds((par * pairs + q) * part, part), :] = vt[
                    q, pl.ds(start, part), pl.ds(par * half, half)
                ]
        if k <= n // 2:
            for j in range(own // 2):
                chunks[k][pl.ds(body + j * ch, ch), :] = jnp.concatenate(
                    [modes[2 * j], modes[2 * j + 1]], axis=1
                )
    tail = body + own // 2 * ch
    for par in range(2):
        lane = pl.ds(par * half, half)
        chunks[1][pl.ds(tail + par * cols, cols), :] = vt[(1 - upper) * (pairs - 1), :, lane]
        odd[pl.ds(par * cols, cols), :] = vt[upper * (pairs - 1), :, lane]


def ends_of(near, odd, cols):
    upper = lax.axis_index("depth") % 2 == 1
    tail = near.shape[0] - 2 * cols
    one = jnp.concatenate([near[pl.ds(tail, cols), :], near[pl.ds(tail + cols, cols), :]], axis=1)
    two = jnp.concatenate([odd[pl.ds(0, cols), :], odd[pl.ds(cols, cols), :]], axis=1)
    one, two = one.astype(F32), two.astype(F32)
    return jnp.where(upper, one, two), jnp.where(upper, two, one)


def strips_kernel(vt, near, odd, even_out, odd_out):
    pairs, cols, _ = vt.shape
    before, after = ends_of(near, odd, cols)
    mids = [before] + [vt[q].astype(F32) for q in range(pairs)] + [after]
    head = jnp.concatenate([m[:2] for m in mids], axis=0)
    tail = jnp.concatenate([m[cols - 2 :] for m in mids], axis=0)
    upper = lax.axis_index("gx") % 2 == 1
    even_out[...] = jnp.where(upper, head, tail).astype(BF)
    odd_out[...] = jnp.where(upper, tail, head).astype(BF)


def basis_into(n, slab, out, out_t):
    shape = out.shape
    own = shape[0] // (2 * n)
    pairs = slab // 2
    core = lax.axis_index("gx") % 2
    row = lax.broadcasted_iota(jnp.int32, shape, 0)
    col = lax.broadcasted_iota(jnp.int32, shape, 1)
    mode_index = jnp.zeros(shape, jnp.int32)
    depth_pos = jnp.zeros(shape, jnp.int32)
    for side in range(2):
        for k in range(n):
            at = (side * n + k) * own
            first = target(k) * (2 * own) + (core if side == 0 else 1 - core) * own
            mode_index = jnp.where(row >= at, first + row - at, mode_index)
            at = (side * n + k) * pairs
            first = target(k) * slab + side
            depth_pos = jnp.where(col >= at, first + 2 * (col - at), depth_pos)
    value = mode_basis(mode_index, depth_pos, slab * n)
    out[...] = value.astype(BF)
    out_t[...] = value.T.astype(BF)


def prepare_kernel(n, slab, first, second, basis, basis_t, out_first, out_second, held, sem):
    ch = first.shape[3]
    loads = [
        pltpu.make_async_copy(src, held.at[i], sem.at[i]) for i, src in enumerate((first, second))
    ]
    for load in loads:
        load.start()
    basis_into(n, slab, basis, basis_t)
    for i, dst in ((0, out_first), (1, out_second)):
        loads[i].wait()
        src = held.at[i]
        for e in range(3):
            block = {}
            for a in range(3):
                for yi in range(2):
                    both = jnp.concatenate([src[a, yi + 1, e], src[a, yi, e]], axis=0)
                    block[a, yi] = both.astype(F32).T.astype(BF)
            for h in range(2):
                for pi in range(2):
                    for po in range(2):
                        a = 2 * h + pi - po
                        for yi in range(2):
                            value = block[a, yi] if 0 <= a <= 2 else jnp.zeros((ch, 2 * ch), BF)
                            dst[
                                e * 2 + h,
                                pl.ds((pi * 2 + yi) * ch, ch),
                                pl.ds(po * 2 * ch, 2 * ch),
                            ] = value


def shifted(dst, index, rows, value):
    n = value.shape[0]
    wide = value.astype(F32)
    dst[1, pl.ds(index * rows, rows), :] = value
    dst[0, pl.ds(index * rows, rows), :] = pltpu.roll(wide, 1, 0).astype(BF)
    dst[2, pl.ds(index * rows, rows), :] = pltpu.roll(wide, n - 1, 0).astype(BF)


def conv_kernel(ngx, n, flat, vt, near, odd, even_edge, odd_edge, w1, w2, out, ext, hid):
    pairs, cols, lanes = vt.shape
    rows = cols + 16
    ch = lanes // 4
    me = lax.axis_index("depth")
    gx = lax.axis_index("gx")
    fill = jnp.zeros((rows - cols - 4, lanes), F32)
    before, after = ends_of(near, odd, cols)
    upper = gx % 2 == 1
    even_side, odd_side = even_edge[...].astype(F32), odd_edge[...].astype(F32)
    left = jnp.where(upper, even_side, odd_side)
    right = jnp.where(upper, odd_side, even_side)
    for q in range(pairs + 2):
        mid = before if q == 0 else after if q == pairs + 1 else vt[q - 1].astype(F32)
        ring = jnp.concatenate(
            [mid, right[2 * q : 2 * q + 2], fill, left[2 * q : 2 * q + 2]], axis=0
        ).astype(BF)
        shifted(ext, q, rows, ring)
    at = lax.broadcasted_iota(jnp.int32, (rows, lanes), 0)
    lane = lax.broadcasted_iota(jnp.int32, (rows, lanes), 1)
    inside = jnp.logical_and(
        jnp.logical_or(at != rows - 1, gx > 0), jnp.logical_or(at != cols, gx < ngx - 1)
    )
    for p in range(pairs + 1):
        acc = jnp.zeros((rows, lanes), F32)
        for e in range(3):
            for h in range(2):
                acc += jnp.dot(
                    ext[e, pl.ds((p + h) * rows, rows), :],
                    w1[e * 2 + h],
                    preferred_element_type=F32,
                )
        keep = inside
        if p == 0:
            keep = jnp.logical_and(keep, jnp.logical_or(lane >= lanes // 2, me > 0))
        if p == pairs:
            keep = jnp.logical_and(keep, jnp.logical_or(lane < lanes // 2, me < n - 1))
        value = jnp.where(keep, jax.nn.gelu(acc), 0.0).astype(BF)
        shifted(hid, p, rows, value)
    for p in range(pairs):
        acc = jnp.zeros((cols, lanes), F32)
        for e in range(3):
            for h in range(2):
                acc += jnp.dot(
                    hid[e, pl.ds((p + h) * rows, cols), :],
                    w2[e * 2 + h],
                    preferred_element_type=F32,
                )
        turned = acc.T
        for j in range(4):
            out[p // 2, pl.ds(4 * (p % 2) + j, ch, stride=8), :] = turned[j * ch : (j + 1) * ch]
        if p % 2 == 1:
            own = flat[:, pl.ds(8 * (p // 2), 8), :].astype(F32)
            out[p // 2] += own.reshape(8 * ch, cols)


def gather_kernel(body, *refs):
    *parts, out = refs
    n, rows, _ = out.shape
    for k in range(n):
        out[k] = parts[k][pl.ds(body if k <= n // 2 else 0, rows), :]


def coef_kernel(part, basis, *refs):
    *chunks, coef, field = refs
    n = len(chunks)
    modes = basis.shape[0]
    steps = basis.shape[1] // 2
    per = steps * part // n
    for k in range(n):
        for par in range(2):
            field[par, pl.ds(k * per, per), :] = chunks[k][pl.ds(par * per, per), :].astype(F32)
    for x in range(part):
        piece = jnp.concatenate(
            [field[par, pl.ds(x, steps, stride=part), :].astype(BF) for par in range(2)], axis=0
        )
        coef[pl.ds(x, modes, stride=part), :] = jnp.dot(
            basis[...], piece, preferred_element_type=F32
        )


def spectral_kernel(part, basis_t, coef, mine, other, *refs):
    n = mine.shape[0]
    outs = refs[:n]
    field, mix = refs[n:]
    modes = basis_t.shape[1]
    steps = basis_t.shape[0] // 2
    per = steps * part // n
    wide = mine.shape[2]
    ch = wide // 2
    low = lax.broadcasted_iota(jnp.int32, (part, wide), 1) < ch
    at = 0
    for side in range(2):
        for k in range(n):
            for j in range(mine.shape[1] // ch):
                w = (mine, other)[side][k, pl.ds(j * ch, ch), :]
                c0 = coef[pl.ds(at * part, part), :]
                c1 = coef[pl.ds((at + 1) * part, part), :]
                lhs = jnp.concatenate(
                    [
                        jnp.where(low, c0, 0.0),
                        jnp.where(low, pltpu.roll(c0, ch, 1), 0.0),
                        jnp.where(low, 0.0, pltpu.roll(c1, ch, 1)),
                        jnp.where(low, 0.0, c1),
                    ],
                    axis=0,
                ).astype(BF)
                r = lax.dot_general(
                    lhs, w, (((1,), (1,)), ((), ())), preferred_element_type=F32
                )
                for t in range(2):
                    mix[pl.ds((at + t) * part, part), :] = jnp.concatenate(
                        [
                            r[2 * t * part : (2 * t + 1) * part],
                            r[(2 * t + 1) * part : (2 * t + 2) * part],
                        ],
                        axis=1,
                    )
                at += 2
    for x in range(part):
        value = jnp.dot(
            basis_t[...],
            mix[pl.ds(x, modes, stride=part), :].astype(BF),
            preferred_element_type=F32,
        )
        for par in range(2):
            field[par, pl.ds(x, steps, stride=part), :] = value[par * steps : (par + 1) * steps]
    for k in range(n):
        for par in range(2):
            outs[k][pl.ds(par * per, per), :] = field[par, pl.ds(k * per, per), :].astype(BF)


def join_kernel(base, *refs):
    *chunks, out, total, wide, done, sem = refs
    pairs, cols, lanes = total.shape
    n = len(chunks)
    part = cols // n
    half = lanes // 2
    ch = lanes // 4
    for k in range(n):
        start = pl.multiple_of(target(k) * part, part)
        for q in range(pairs):
            for par in range(2):
                total[q, pl.ds(start, part), pl.ds(par * half, half)] = chunks[k][
                    pl.ds((par * pairs + q) * part, part), :
                ]
    stores = []
    for g in range(pairs // 2):
        for i in range(2):
            turned = total[2 * g + i].T.astype(F32)
            for j in range(4):
                wide[g, pl.ds(4 * i + j, ch, stride=8), :] = turned[j * ch : (j + 1) * ch]
        done[g] = (base[g] + wide[g]).reshape(ch, 8, cols).astype(BF)
        stores.append(
            pltpu.make_async_copy(done.at[g], out.at[:, pl.ds(8 * g, 8), :], sem.at[g])
        )
        stores[g].start()
    for store in stores:
        store.wait()


def swap(value, axis, k):
    count = lax.axis_size(axis)
    return lax.ppermute(value, axis, [(i, i ^ k) for i in range(count) if i ^ k < count])


def swap_odd(value, axis):
    pairs = []
    for i in range(1, lax.axis_size(axis) - 1, 2):
        pairs += [(i, i + 1), (i + 1, i)]
    return lax.ppermute(value, axis, pairs)


def block(volume, conv_first, conv_second, mode_weights):
    ch, slab, ny, cols = volume.shape
    n = lax.axis_size("depth")
    ngx = lax.axis_size("gx")
    assert n & (n - 1) == 0 and n > 2 and ngx % 2 == 0
    pairs = slab // 2
    lanes = 2 * ny * ch
    half = lanes // 2
    part = cols // n
    per = pairs * part
    modes = mode_weights.shape[0] * n
    wrows = mode_weights.shape[0] // 4 * ch
    total_z = slab * n

    flat = volume.reshape(ch * slab * ny, cols)
    sizes = [
        2 * per + (wrows if k <= n // 2 else 0) + (2 * cols if k == 1 else 0) for k in range(n)
    ]
    vt, odd, *chunks = pl.pallas_call(
        functools.partial(split_kernel, slab),
        out_shape=[
            jax.ShapeDtypeStruct((pairs, cols, lanes), BF),
            jax.ShapeDtypeStruct((2 * cols, half), BF),
        ]
        + [jax.ShapeDtypeStruct((size, half), BF) for size in sizes],
        in_specs=[HBM, HBM],
        out_specs=[VMEM] * (n + 2),
        scratch_shapes=[
            pltpu.VMEM(flat.shape, BF),
            pltpu.VMEM((mode_weights.shape[0] // 2,) + mode_weights.shape[1:], BF),
            pltpu.VMEM(flat.shape, F32),
            pltpu.SemaphoreType.DMA((5,)),
        ],
        compiler_params=params(),
        cost_estimate=cost(0, 3 * volume.size * 2),
    )(in_hbm(flat), in_hbm(mode_weights))
    got = [chunks[0]] + [swap(chunks[k], "depth", k) for k in range(1, n)]
    odd = swap_odd(odd, "depth")

    body = slice(2 * per, 2 * per + wrows)
    far = got[n // 2][body]
    passed = [swap(far, "depth", k) for k in range(1, n // 2)]
    mine = pl.pallas_call(
        functools.partial(gather_kernel, 2 * per),
        out_shape=jax.ShapeDtypeStruct((n, wrows, half), BF),
        in_specs=[VMEM] * n,
        out_specs=VMEM,
        compiler_params=params(),
        cost_estimate=cost(0, n * wrows * half * 4),
    )(*got[: n // 2 + 1], *passed)
    other = swap(mine, "gx", 1)

    basis, basis_t, w1, w2 = pl.pallas_call(
        functools.partial(prepare_kernel, n, slab),
        out_shape=[
            jax.ShapeDtypeStruct((modes, total_z), BF),
            jax.ShapeDtypeStruct((total_z, modes), BF),
        ]
        + [jax.ShapeDtypeStruct((6, lanes, lanes), BF)] * 2,
        in_specs=[HBM, HBM],
        out_specs=[VMEM] * 4,
        scratch_shapes=[
            pltpu.VMEM((2,) + conv_first.shape, BF),
            pltpu.SemaphoreType.DMA((2,)),
        ],
        compiler_params=params(),
        cost_estimate=cost(0, 4 * conv_first.size * 2 * 4),
    )(in_hbm(conv_first), in_hbm(conv_second))
    even_edge, odd_edge = pl.pallas_call(
        strips_kernel,
        out_shape=[jax.ShapeDtypeStruct((2 * (pairs + 2), lanes), BF)] * 2,
        in_specs=[VMEM] * 3,
        out_specs=[VMEM] * 2,
        compiler_params=params(),
        cost_estimate=cost(0, 8 * pairs * lanes * 4),
    )(vt, got[1], odd)
    even_edge = swap(even_edge, "gx", 1)
    odd_edge = swap_odd(odd_edge, "gx")

    coef = pl.pallas_call(
        functools.partial(coef_kernel, part),
        out_shape=jax.ShapeDtypeStruct((modes * part, half), F32),
        in_specs=[VMEM] * (1 + n),
        out_specs=VMEM,
        scratch_shapes=[pltpu.VMEM((2, n * per, half), F32)],
        compiler_params=params(),
        cost_estimate=cost(2 * modes * total_z * part * half, 2 * volume.size * 2),
    )(basis, *got)
    outs = pl.pallas_call(
        functools.partial(spectral_kernel, part),
        out_shape=[jax.ShapeDtypeStruct((2 * per, half), BF)] * n,
        in_specs=[VMEM] * 4,
        out_specs=[VMEM] * n,
        scratch_shapes=[pltpu.VMEM((2, n * per, half), F32), pltpu.VMEM((modes * part, half), F32)],
        compiler_params=params(),
        cost_estimate=cost(4 * modes * total_z * part * half, 2 * volume.size * 2),
    )(basis_t, coef, mine, other)
    spec = [outs[0]] + [swap(outs[k], "depth", k) for k in range(1, n)]

    base = pl.pallas_call(
        functools.partial(conv_kernel, ngx, n),
        out_shape=jax.ShapeDtypeStruct((pairs // 2, 8 * ch, cols), F32),
        in_specs=[VMEM] * 8,
        out_specs=VMEM,
        scratch_shapes=[
            pltpu.VMEM((3, (pairs + 2) * (cols + 16), lanes), BF),
            pltpu.VMEM((3, (pairs + 1) * (cols + 16), lanes), BF),
        ],
        compiler_params=params(),
        cost_estimate=cost(4 * 6 * pairs * cols * lanes * lanes, volume.size * 8),
    )(flat.reshape(ch, slab * ny, cols), vt, got[1], odd, even_edge, odd_edge, w1, w2)

    out = pl.pallas_call(
        join_kernel,
        out_shape=jax.ShapeDtypeStruct((ch, slab * ny, cols), BF),
        in_specs=[VMEM] * (1 + n),
        out_specs=HBM,
        scratch_shapes=[
            pltpu.VMEM((pairs, cols, lanes), BF),
            pltpu.VMEM((pairs // 2, 8 * ch, cols), F32),
            pltpu.VMEM((pairs // 2, ch, 8, cols), BF),
            pltpu.SemaphoreType.DMA((pairs // 2,)),
        ],
        compiler_params=params(),
        cost_estimate=cost(0, volume.size * 10),
    )(base, *spec)
    return out.reshape(volume.shape)


def solution(mesh):
    placed = (P(None, "depth", None, "gx"), P(), P(), P("depth", None, None))
    return jax.shard_map(
        block, mesh=mesh, in_specs=placed, out_specs=P(None, "depth", None, "gx"), check_vma=False
    )
```

```python
import functools
import math

import jax
import jax.numpy as jnp
from jax import lax
from jax.experimental import pallas as pl
from jax.experimental.pallas import tpu as pltpu
from jax.sharding import PartitionSpec as P


MODES = 32
BF = jnp.bfloat16
F32 = jnp.float32
VMEM = pl.BlockSpec(memory_space=pltpu.VMEM)
HBM = pl.BlockSpec(memory_space=pltpu.HBM)


def mode_basis(mode_index, depth_pos, total_z):
    frequency = jnp.where(mode_index < MODES, mode_index, mode_index - MODES + 1).astype(F32)
    odd_steps = (2 * depth_pos + 1).astype(F32)
    angles = frequency * odd_steps * (math.pi / (2.0 * total_z))
    values = jnp.where(mode_index < MODES, jnp.cos(angles), jnp.sin(angles))
    return values * math.sqrt(2.0 / total_z)


def cost(flops, nbytes, trans=0):
    return pl.CostEstimate(flops=flops, bytes_accessed=nbytes, transcendentals=trans)


def in_hbm(value):
    return pltpu.with_memory_space_constraint(value, pltpu.HBM)


def params():
    return pltpu.CompilerParams(vmem_limit_bytes=20 * 1024 * 1024)


def target(k):
    me = lax.axis_index("depth")
    return me ^ k


def split_kernel(slab, flat, weights, vt, odd, *refs):
    *chunks, held, modes, wide, sem = refs
    pairs, cols, lanes = vt.shape
    n = len(chunks)
    part = cols // n
    half = lanes // 2
    own = weights.shape[0] // 2
    ch = weights.shape[2]
    ny = flat.shape[1] // slab
    deep = 4 * ny
    core = lax.axis_index("gx") % 2
    upper = lax.axis_index("depth") % 2
    groups = pairs // 2
    loads = [
        pltpu.make_async_copy(flat.at[:, pl.ds(deep * g, deep), :], held.at[g], sem.at[g])
        for g in range(groups)
    ]
    loads.append(
        pltpu.make_async_copy(weights.at[pl.ds(core * own, own)], modes, sem.at[groups])
    )
    for load in loads:
        load.start()
    for g in range(groups):
        loads[g].wait()
        wide[g] = held[g].astype(F32).reshape(deep * ch, cols)
        for i in range(2):
            rows = [wide[g, pl.ds(2 * ny * i + j, ch, stride=deep), :] for j in range(2 * ny)]
            vt[2 * g + i] = jnp.concatenate(rows, axis=0).astype(BF).T
    body = 2 * pairs * part
    loads[groups].wait()
    for k in range(n):
        start = pl.multiple_of(target(k) * part, part)
        for q in range(pairs):
            for par in range(2):
                chunks[k][pl.ds((par * pairs + q) * part, part), :] = vt[
                    q, pl.ds(start, part), pl.ds(par * half, half)
                ]
        if k <= n // 2:
            for j in range(own // 2):
                chunks[k][pl.ds(body + j * ch, ch), :] = jnp.concatenate(
                    [modes[2 * j], modes[2 * j + 1]], axis=1
                )
    tail = body + own // 2 * ch
    for par in range(2):
        lane = pl.ds(par * half, half)
        chunks[1][pl.ds(tail + par * cols, cols), :] = vt[(1 - upper) * (pairs - 1), :, lane]
        odd[pl.ds(par * cols, cols), :] = vt[upper * (pairs - 1), :, lane]


def ends_of(near, odd, cols):
    upper = lax.axis_index("depth") % 2 == 1
    tail = near.shape[0] - 2 * cols
    one = jnp.concatenate([near[pl.ds(tail, cols), :], near[pl.ds(tail + cols, cols), :]], axis=1)
    two = jnp.concatenate([odd[pl.ds(0, cols), :], odd[pl.ds(cols, cols), :]], axis=1)
    one, two = one.astype(F32), two.astype(F32)
    return jnp.where(upper, one, two), jnp.where(upper, two, one)


def strips_kernel(vt, near, odd, even_out, odd_out):
    pairs, cols, _ = vt.shape
    before, after = ends_of(near, odd, cols)
    mids = [before] + [vt[q].astype(F32) for q in range(pairs)] + [after]
    head = jnp.concatenate([m[:2] for m in mids], axis=0)
    tail = jnp.concatenate([m[cols - 2 :] for m in mids], axis=0)
    upper = lax.axis_index("gx") % 2 == 1
    even_out[...] = jnp.where(upper, head, tail).astype(BF)
    odd_out[...] = jnp.where(upper, tail, head).astype(BF)


def basis_into(n, slab, out, out_t):
    shape = out.shape
    own = shape[0] // (2 * n)
    pairs = slab // 2
    core = lax.axis_index("gx") % 2
    row = lax.broadcasted_iota(jnp.int32, shape, 0)
    col = lax.broadcasted_iota(jnp.int32, shape, 1)
    mode_index = jnp.zeros(shape, jnp.int32)
    depth_pos = jnp.zeros(shape, jnp.int32)
    for side in range(2):
        for k in range(n):
            at = (side * n + k) * own
            first = target(k) * (2 * own) + (core if side == 0 else 1 - core) * own
            mode_index = jnp.where(row >= at, first + row - at, mode_index)
            at = (side * n + k) * pairs
            first = target(k) * slab + side
            depth_pos = jnp.where(col >= at, first + 2 * (col - at), depth_pos)
    value = mode_basis(mode_index, depth_pos, slab * n)
    out[...] = value.astype(BF)
    out_t[...] = value.T.astype(BF)


def prepare_kernel(n, slab, first, second, basis, basis_t, out_first, out_second, held, sem):
    ch = first.shape[3]
    loads = [
        pltpu.make_async_copy(src, held.at[i], sem.at[i]) for i, src in enumerate((first, second))
    ]
    for load in loads:
        load.start()
    basis_into(n, slab, basis, basis_t)
    for i, dst in ((0, out_first), (1, out_second)):
        loads[i].wait()
        src = held.at[i]
        for e in range(3):
            block = {}
            for a in range(3):
                for yi in range(2):
                    both = jnp.concatenate([src[a, yi + 1, e], src[a, yi, e]], axis=0)
                    block[a, yi] = both.astype(F32).T.astype(BF)
            for h in range(2):
                for pi in range(2):
                    for po in range(2):
                        a = 2 * h + pi - po
                        for yi in range(2):
                            value = block[a, yi] if 0 <= a <= 2 else jnp.zeros((ch, 2 * ch), BF)
                            dst[
                                e * 2 + h,
                                pl.ds((pi * 2 + yi) * ch, ch),
                                pl.ds(po * 2 * ch, 2 * ch),
                            ] = value


def shifted(dst, index, rows, value):
    n = value.shape[0]
    wide = value.astype(F32)
    dst[1, pl.ds(index * rows, rows), :] = value
    dst[0, pl.ds(index * rows, rows), :] = pltpu.roll(wide, 1, 0).astype(BF)
    dst[2, pl.ds(index * rows, rows), :] = pltpu.roll(wide, n - 1, 0).astype(BF)


def conv_kernel(ngx, n, flat, vt, near, odd, even_edge, odd_edge, w1, w2, out, ext, hid):
    pairs, cols, lanes = vt.shape
    rows = cols + 16
    ch = lanes // 4
    me = lax.axis_index("depth")
    gx = lax.axis_index("gx")
    fill = jnp.zeros((rows - cols - 4, lanes), F32)
    before, after = ends_of(near, odd, cols)
    upper = gx % 2 == 1
    even_side, odd_side = even_edge[...].astype(F32), odd_edge[...].astype(F32)
    left = jnp.where(upper, even_side, odd_side)
    right = jnp.where(upper, odd_side, even_side)
    for q in range(pairs + 2):
        mid = before if q == 0 else after if q == pairs + 1 else vt[q - 1].astype(F32)
        ring = jnp.concatenate(
            [mid, right[2 * q : 2 * q + 2], fill, left[2 * q : 2 * q + 2]], axis=0
        ).astype(BF)
        shifted(ext, q, rows, ring)
    at = lax.broadcasted_iota(jnp.int32, (rows, lanes), 0)
    lane = lax.broadcasted_iota(jnp.int32, (rows, lanes), 1)
    inside = jnp.logical_and(
        jnp.logical_or(at != rows - 1, gx > 0), jnp.logical_or(at != cols, gx < ngx - 1)
    )
    for p in range(pairs + 1):
        acc = jnp.zeros((rows, lanes), F32)
        for e in range(3):
            for h in range(2):
                acc += jnp.dot(
                    ext[e, pl.ds((p + h) * rows, rows), :],
                    w1[e * 2 + h],
                    preferred_element_type=F32,
                )
        keep = inside
        if p == 0:
            keep = jnp.logical_and(keep, jnp.logical_or(lane >= lanes // 2, me > 0))
        if p == pairs:
            keep = jnp.logical_and(keep, jnp.logical_or(lane < lanes // 2, me < n - 1))
        value = jnp.where(keep, jax.nn.gelu(acc), 0.0).astype(BF)
        shifted(hid, p, rows, value)
    for p in range(pairs):
        acc = jnp.zeros((cols, lanes), F32)
        for e in range(3):
            for h in range(2):
                acc += jnp.dot(
                    hid[e, pl.ds((p + h) * rows, cols), :],
                    w2[e * 2 + h],
                    preferred_element_type=F32,
                )
        turned = acc.T
        for j in range(4):
            out[p // 2, pl.ds(4 * (p % 2) + j, ch, stride=8), :] = turned[j * ch : (j + 1) * ch]
        if p % 2 == 1:
            own = flat[:, pl.ds(8 * (p // 2), 8), :].astype(F32)
            out[p // 2] += own.reshape(8 * ch, cols)


def gather_kernel(body, *refs):
    *parts, out = refs
    n, rows, _ = out.shape
    for k in range(n):
        out[k] = parts[k][pl.ds(body if k <= n // 2 else 0, rows), :]


def coef_kernel(part, basis, *refs):
    *chunks, coef, field = refs
    n = len(chunks)
    modes = basis.shape[0]
    steps = basis.shape[1] // 2
    per = steps * part // n
    for k in range(n):
        for par in range(2):
            field[par, pl.ds(k * per, per), :] = chunks[k][pl.ds(par * per, per), :].astype(F32)
    for x in range(part):
        piece = jnp.concatenate(
            [field[par, pl.ds(x, steps, stride=part), :].astype(BF) for par in range(2)], axis=0
        )
        coef[pl.ds(x, modes, stride=part), :] = jnp.dot(
            basis[...], piece, preferred_element_type=F32
        )


def spectral_kernel(part, basis_t, coef, mine, other, *refs):
    n = mine.shape[0]
    outs = refs[:n]
    field, mix = refs[n:]
    modes = basis_t.shape[1]
    steps = basis_t.shape[0] // 2
    per = steps * part // n
    wide = mine.shape[2]
    ch = wide // 2
    low = lax.broadcasted_iota(jnp.int32, (part, wide), 1) < ch
    at = 0
    for side in range(2):
        for k in range(n):
            for j in range(mine.shape[1] // ch):
                w = (mine, other)[side][k, pl.ds(j * ch, ch), :]
                c0 = coef[pl.ds(at * part, part), :]
                c1 = coef[pl.ds((at + 1) * part, part), :]
                lhs = jnp.concatenate(
                    [
                        jnp.where(low, c0, 0.0),
                        jnp.where(low, pltpu.roll(c0, ch, 1), 0.0),
                        jnp.where(low, 0.0, pltpu.roll(c1, ch, 1)),
                        jnp.where(low, 0.0, c1),
                    ],
                    axis=0,
                ).astype(BF)
                r = lax.dot_general(
                    lhs, w, (((1,), (1,)), ((), ())), preferred_element_type=F32
                )
                for t in range(2):
                    mix[pl.ds((at + t) * part, part), :] = jnp.concatenate(
                        [
                            r[2 * t * part : (2 * t + 1) * part],
                            r[(2 * t + 1) * part : (2 * t + 2) * part],
                        ],
                        axis=1,
                    )
                at += 2
    for x in range(part):
        value = jnp.dot(
            basis_t[...],
            mix[pl.ds(x, modes, stride=part), :].astype(BF),
            preferred_element_type=F32,
        )
        for par in range(2):
            field[par, pl.ds(x, steps, stride=part), :] = value[par * steps : (par + 1) * steps]
    for k in range(n):
        for par in range(2):
            outs[k][pl.ds(par * per, per), :] = field[par, pl.ds(k * per, per), :].astype(BF)


def join_kernel(base, *refs):
    *chunks, out, total, wide, done, sem = refs
    pairs, cols, lanes = total.shape
    n = len(chunks)
    part = cols // n
    half = lanes // 2
    ch = lanes // 4
    stores = []
    for g in range(pairs // 2):
        for i in range(2):
            q = 2 * g + i
            for k in range(n):
                start = pl.multiple_of(target(k) * part, part)
                for par in range(2):
                    total[q, pl.ds(start, part), pl.ds(par * half, half)] = chunks[k][
                        pl.ds((par * pairs + q) * part, part), :
                    ]
            turned = total[q].T.astype(F32)
            for j in range(4):
                wide[g, pl.ds(4 * i + j, ch, stride=8), :] = turned[j * ch : (j + 1) * ch]
        done[g] = (base[g] + wide[g]).reshape(ch, 8, cols).astype(BF)
        stores.append(
            pltpu.make_async_copy(done.at[g], out.at[:, pl.ds(8 * g, 8), :], sem.at[g])
        )
        stores[g].start()
    for store in stores:
        store.wait()


def swap(value, axis, k):
    count = lax.axis_size(axis)
    return lax.ppermute(value, axis, [(i, i ^ k) for i in range(count) if i ^ k < count])


def swap_odd(value, axis):
    pairs = []
    for i in range(1, lax.axis_size(axis) - 1, 2):
        pairs += [(i, i + 1), (i + 1, i)]
    return lax.ppermute(value, axis, pairs)


def block(volume, conv_first, conv_second, mode_weights):
    ch, slab, ny, cols = volume.shape
    n = lax.axis_size("depth")
    ngx = lax.axis_size("gx")
    assert n & (n - 1) == 0 and n > 2 and ngx % 2 == 0
    pairs = slab // 2
    lanes = 2 * ny * ch
    half = lanes // 2
    part = cols // n
    per = pairs * part
    modes = mode_weights.shape[0] * n
    wrows = mode_weights.shape[0] // 4 * ch
    total_z = slab * n

    flat = volume.reshape(ch, slab * ny, cols)
    sizes = [
        2 * per + (wrows if k <= n // 2 else 0) + (2 * cols if k == 1 else 0) for k in range(n)
    ]
    vt, odd, *chunks = pl.pallas_call(
        functools.partial(split_kernel, slab),
        out_shape=[
            jax.ShapeDtypeStruct((pairs, cols, lanes), BF),
            jax.ShapeDtypeStruct((2 * cols, half), BF),
        ]
        + [jax.ShapeDtypeStruct((size, half), BF) for size in sizes],
        in_specs=[HBM, HBM],
        out_specs=[VMEM] * (n + 2),
        scratch_shapes=[
            pltpu.VMEM((pairs // 2, ch, 4 * ny, cols), BF),
            pltpu.VMEM((mode_weights.shape[0] // 2,) + mode_weights.shape[1:], BF),
            pltpu.VMEM((pairs // 2, ch * 4 * ny, cols), F32),
            pltpu.SemaphoreType.DMA((pairs // 2 + 1,)),
        ],
        compiler_params=params(),
        cost_estimate=cost(0, 3 * volume.size * 2),
    )(in_hbm(flat), in_hbm(mode_weights))
    got = [chunks[0]] + [swap(chunks[k], "depth", k) for k in range(1, n)]
    odd = swap_odd(odd, "depth")

    body = slice(2 * per, 2 * per + wrows)
    far = got[n // 2][body]
    passed = [swap(far, "depth", k) for k in range(1, n // 2)]
    mine = pl.pallas_call(
        functools.partial(gather_kernel, 2 * per),
        out_shape=jax.ShapeDtypeStruct((n, wrows, half), BF),
        in_specs=[VMEM] * n,
        out_specs=VMEM,
        compiler_params=params(),
        cost_estimate=cost(0, n * wrows * half * 4),
    )(*got[: n // 2 + 1], *passed)
    other = swap(mine, "gx", 1)

    basis, basis_t, w1, w2 = pl.pallas_call(
        functools.partial(prepare_kernel, n, slab),
        out_shape=[
            jax.ShapeDtypeStruct((modes, total_z), BF),
            jax.ShapeDtypeStruct((total_z, modes), BF),
        ]
        + [jax.ShapeDtypeStruct((6, lanes, lanes), BF)] * 2,
        in_specs=[HBM, HBM],
        out_specs=[VMEM] * 4,
        scratch_shapes=[
            pltpu.VMEM((2,) + conv_first.shape, BF),
            pltpu.SemaphoreType.DMA((2,)),
        ],
        compiler_params=params(),
        cost_estimate=cost(0, 4 * conv_first.size * 2 * 4),
    )(in_hbm(conv_first), in_hbm(conv_second))
    even_edge, odd_edge = pl.pallas_call(
        strips_kernel,
        out_shape=[jax.ShapeDtypeStruct((2 * (pairs + 2), lanes), BF)] * 2,
        in_specs=[VMEM] * 3,
        out_specs=[VMEM] * 2,
        compiler_params=params(),
        cost_estimate=cost(0, 8 * pairs * lanes * 4),
    )(vt, got[1], odd)
    even_edge = swap(even_edge, "gx", 1)
    odd_edge = swap_odd(odd_edge, "gx")

    coef = pl.pallas_call(
        functools.partial(coef_kernel, part),
        out_shape=jax.ShapeDtypeStruct((modes * part, half), F32),
        in_specs=[VMEM] * (1 + n),
        out_specs=VMEM,
        scratch_shapes=[pltpu.VMEM((2, n * per, half), F32)],
        compiler_params=params(),
        cost_estimate=cost(2 * modes * total_z * part * half, 2 * volume.size * 2),
    )(basis, *got)
    outs = pl.pallas_call(
        functools.partial(spectral_kernel, part),
        out_shape=[jax.ShapeDtypeStruct((2 * per, half), BF)] * n,
        in_specs=[VMEM] * 4,
        out_specs=[VMEM] * n,
        scratch_shapes=[pltpu.VMEM((2, n * per, half), F32), pltpu.VMEM((modes * part, half), F32)],
        compiler_params=params(),
        cost_estimate=cost(4 * modes * total_z * part * half, 2 * volume.size * 2),
    )(basis_t, coef, mine, other)
    spec = [outs[0]] + [swap(outs[k], "depth", k) for k in range(1, n)]

    base = pl.pallas_call(
        functools.partial(conv_kernel, ngx, n),
        out_shape=jax.ShapeDtypeStruct((pairs // 2, 8 * ch, cols), F32),
        in_specs=[VMEM] * 8,
        out_specs=VMEM,
        scratch_shapes=[
            pltpu.VMEM((3, (pairs + 2) * (cols + 16), lanes), BF),
            pltpu.VMEM((3, (pairs + 1) * (cols + 16), lanes), BF),
        ],
        compiler_params=params(),
        cost_estimate=cost(4 * 6 * pairs * cols * lanes * lanes, volume.size * 8),
    )(flat, vt, got[1], odd, even_edge, odd_edge, w1, w2)

    out = pl.pallas_call(
        join_kernel,
        out_shape=jax.ShapeDtypeStruct((ch, slab * ny, cols), BF),
        in_specs=[VMEM] * (1 + n),
        out_specs=HBM,
        scratch_shapes=[
            pltpu.VMEM((pairs, cols, lanes), BF),
            pltpu.VMEM((pairs // 2, 8 * ch, cols), F32),
            pltpu.VMEM((pairs // 2, ch, 8, cols), BF),
            pltpu.SemaphoreType.DMA((pairs // 2,)),
        ],
        compiler_params=params(),
        cost_estimate=cost(0, volume.size * 10),
    )(base, *spec)
    return out.reshape(volume.shape)


def solution(mesh):
    placed = (P(None, "depth", None, "gx"), P(), P(), P("depth", None, None))
    return jax.shard_map(
        block, mesh=mesh, in_specs=placed, out_specs=P(None, "depth", None, "gx"), check_vma=False
    )
```
